32 devices in a mesh: group: 2 (over y), scen: 16 (over z, x, core).
Axes of the slice: x: 2, y: 2, z: 4, core: 2. Of those that a mesh axis runs over, the one named last changes fastest.
Arguments:
- scenario_rows: bfloat16 [32, 2048, 2048], P(('group', 'scen')), parts along dimension 0, may hold values from -1 to 1
- barrier: float32 [32, 2048], P(('group', 'scen')), parts along dimension 0, may hold values from 0.01 to 61
- blocks: int32 [32, 6], P(('group', 'scen')), parts along dimension 0, may hold values from 0 to 15, all different within a row
- link_diag: float32 [4096], P('group'), parts along dimension 0, may hold values from 0.2 to 2
Outputs:
- factor: float32 [256, 16, 1024], P('group', 'scen'), parts along dimension 0
- trailing: float32 [128, 16, 1024], P('group', 'scen'), parts along dimension 0
The draws below stay inside these ranges and needn't reach their ends.
There are 2 independent parts, one for each index of `group`. The reference program is written for one: setup_inputs(seed, part) draws one part's arguments, and reference() takes and returns one part's arrays. A program takes and returns all parts, laid end to end along the dimension named above; each array names one. Nothing has to cross between parts.
Inputs may be any that keep to these rules, and one draw needn't show every extreme that they name: Each row names 6 distinct column blocks, and every block is named by some scenario.
All inputs are finite; a program needn't handle non-finite values.
Results may differ from the reference program's by a relative error of at most 0.0007.
Values sent between devices are 32-bit elements; how exact they have to be, the bound alone decides.
A program may use at most 128 MiB of HBM per device.

```python
import math
import jax
import jax.numpy as jnp
from jax import lax

K_DEV = 2048
BW = 128
NZB = 6
ROWS = 2048
SCENS = 16
N_SCEN = 16


def draw_barrier(key, part):
    common = jnp.exp(jax.random.uniform(jax.random.fold_in(key, 11), (K_DEV,), jnp.float32, math.log(0.03), math.log(30.0)))
    own = jnp.exp(jax.random.uniform(jax.random.fold_in(key, 12), (SCENS, K_DEV), jnp.float32, math.log(0.5), math.log(2.0)))
    return (common[None, :] * own).astype(jnp.float32)


def draw_scenario_rows(key, part):
    cover = SCENS * NZB * BW / ROWS
    unit = 1.0 / (cover * K_DEV * 4.7)
    common_scale = math.sqrt(unit)
    noise_scale = math.sqrt(0.5 * unit)
    base = jax.random.truncated_normal(jax.random.fold_in(key, 7), -4.0, 4.0, (K_DEV, ROWS), jnp.float32)
    noise = jax.random.truncated_normal(jax.random.fold_in(key, 8), -4.0, 4.0, (SCENS, K_DEV, ROWS), jnp.float32)
    values = common_scale * base[None, :, :] + noise_scale * noise
    return values.astype(jnp.bfloat16)


def distinct(own_key, rows, number_of, top, lift):
    ranking = jax.random.permutation(jax.random.fold_in(own_key, 1), number_of)
    boost = ranking
    for power in range(3):
        boost = boost * boost // number_of
    boost = boost * lift // number_of
    chance = jax.random.randint(jax.random.fold_in(own_key, 2), (rows, number_of), 0, 4096) + boost
    holders = jax.random.permutation(jax.random.fold_in(own_key, 3), rows)[jnp.arange(number_of) % rows]
    chance = jnp.where(jnp.arange(rows)[:, None] == holders[None, :], 1 << 14, chance)
    merit = chance * number_of + jnp.arange(number_of)
    return lax.top_k(merit.astype(jnp.int32), top)[1].astype(jnp.int32)


def setup_inputs(seed: int = 0, part: int = 0) -> dict:
    keys = jax.random.split(jax.random.key(seed), 5)
    part_keys = jax.random.split(jax.random.fold_in(keys[4], part), 5)
    scenario_rows = draw_scenario_rows(jax.random.fold_in(jax.random.fold_in(keys[4], part), 71), part)
    barrier = draw_barrier(jax.random.fold_in(jax.random.fold_in(keys[4], part), 71), part)
    blocks = distinct(part_keys[2], SCENS, ROWS // BW, NZB, 0)
    link_diag = jnp.clip(jnp.exp(jax.random.uniform(part_keys[3], (ROWS,), jnp.float32, math.log(0.2), math.log(2.0))), 0.2, 2.0)
    return {"scenario_rows": scenario_rows, "barrier": barrier, "blocks": blocks, "link_diag": link_diag}


def reference(scenario_rows, barrier, blocks, link_diag):
    rows_all = scenario_rows.shape[2]
    panel = rows_all // 2
    half = panel // 2
    column_block = jnp.arange(rows_all, dtype=jnp.int32) // BW

    def accumulate(carry, item):
        coupling, weights, listed = item
        keep = jnp.any(column_block[:, None] == listed[None, :], axis=1)
        masked = jnp.where(keep[None, :], coupling, jnp.zeros_like(coupling))
        weighted = (weights[:, None] * masked.astype(jnp.float32)).astype(jnp.bfloat16)
        left = weighted.astype(jnp.float32)
        right = masked.astype(jnp.float32)
        first = carry[0] + jnp.dot(left.T, right[:, :panel], precision=lax.Precision.HIGHEST)
        second = carry[1] + jnp.dot(left[:, panel:].T, right[:, panel:], precision=lax.Precision.HIGHEST)
        return ((first, second), None)
    start = (jnp.zeros((rows_all, panel), jnp.float32), jnp.zeros((panel, panel), jnp.float32))
    (first, second), unused = lax.scan(accumulate, start, (scenario_rows, barrier, blocks))
    first = first + jnp.concatenate([jnp.diag(link_diag[:panel]), jnp.zeros((panel, panel), jnp.float32)], axis=0)
    second = second + jnp.diag(link_diag[panel:])
    low_one = jnp.linalg.cholesky(first[:half, :half])
    rest_one = jax.scipy.linalg.solve_triangular(low_one, first[half:, :half].T, lower=True).T
    reduced = first[half:, half:] - jnp.dot(rest_one, rest_one[:half].T, precision=lax.Precision.HIGHEST)
    low_two = jnp.linalg.cholesky(reduced[:half])
    rest_two = jax.scipy.linalg.solve_triangular(low_two, reduced[half:].T, lower=True).T
    top = jnp.concatenate([low_one, jnp.zeros((half, half), jnp.float32)], axis=1)
    middle = jnp.concatenate([rest_one[:half], low_two], axis=1)
    bottom = jnp.concatenate([rest_one[half:], rest_two], axis=1)
    factor = jnp.concatenate([top, middle, bottom], axis=0)
    lower_rows = factor[panel:]
    trailing = second - jnp.dot(lower_rows, lower_rows.T, precision=lax.Precision.HIGHEST)
    return (factor.reshape(rows_all // N_SCEN, N_SCEN, panel), trailing.reshape(panel // N_SCEN, N_SCEN, panel))
```

```python
import functools

import jax
import jax.numpy as jnp
from jax import lax
from jax.experimental import pallas as pl
from jax.experimental.pallas import tpu as pltpu
from jax.sharding import PartitionSpec as P

BW = 128
WIDTH = 8
MESH = pl.DeviceIdType.MESH


def halves(value):
    high = value.astype(jnp.bfloat16)
    return high, (value - high.astype(jnp.float32)).astype(jnp.bfloat16)


def contract(left, right, dims):
    lh, ll = halves(left)
    rh, rl = halves(right)
    dot = functools.partial(
        lax.dot_general, dimension_numbers=(dims, ((), ())), preferred_element_type=jnp.float32
    )
    cross = dot(jnp.concatenate([lh, ll], axis=dims[0][0]), jnp.concatenate([rl, rh], axis=dims[1][0]))
    return dot(lh, rh) + cross


def triangle(n):
    return n * (n + 1) // 2


def gram_kernel(listed, coupling, weights, out, table, columns, lefts, whole, arrived, *, touched, count):
    depth, rows_all = coupling.shape
    each = BW // count
    blocks = rows_all // BW
    names = [listed[0, i] for i in range(touched)]
    for end in range(touched - 1, 0, -1):
        for i in range(end):
            names[i], names[i + 1] = jnp.minimum(names[i], names[i + 1]), jnp.maximum(names[i], names[i + 1])
    copies = []
    for i in range(touched):
        copy = pltpu.make_async_copy(
            coupling.at[:, pl.ds(pl.multiple_of(names[i] * BW, BW), BW)],
            columns.at[:, pl.ds(i * BW, BW)],
            arrived.at[i],
        )
        copy.start()
        copies.append(copy)
    lower, upper = triangle(touched), triangle(touched - 1)
    lane = lax.broadcasted_iota(jnp.int32, (1, BW), 1)
    index = jnp.where(lane < blocks, lower, jnp.where(lane < 2 * blocks, lower + touched + 1, 0))
    index = jnp.where((lane >= 2 * blocks) & (lane < 3 * blocks), upper, index)
    index = jnp.where((lane >= 3 * blocks) & (lane < 4 * blocks), upper + touched, index)
    for i in range(touched):
        index = jnp.where(lane == names[i], triangle(i), index)
        index = jnp.where(lane == names[i] + blocks, i, index)
        index = jnp.where(lane == names[i] + 2 * blocks, triangle(i - 1) if i else 0, index)
        index = jnp.where(lane == names[i] + 3 * blocks, i, index)
    table[...] = index
    dot = functools.partial(lax.dot_general, preferred_element_type=jnp.float32)
    pair = 2 if touched % 2 == 0 else 1
    for first in range(0, touched, pair):
        lo, hi = first * BW, (first + pair) * BW
        for i in range(first, first + pair):
            copies[i].wait()
        turned = columns[:, lo:hi].T
        lefts[lo:hi, :] = (weights[...] * turned.astype(jnp.float32)).astype(jnp.bfloat16)
        row = dot(lefts[lo:hi, :], columns[:, :hi], (((1,), (0,)), ((), ())))
        for j in range(first + pair):
            whole[j, lo:hi, :] = row[:, j * BW : (j + 1) * BW]
        if lo:
            column = dot(lefts[:lo, :], columns[:, lo:hi], (((1,), (0,)), ((), ())))
            for j in range(pair):
                whole[first + j, :lo, :] = column[:, j * BW : (j + 1) * BW]
    half = blocks // 4
    for i in range(touched):
        for j in range(i + 1):
            same = (names[i] // half == names[j] // half) & (names[i] < 2 * half)
            share = jnp.where(same, 0.5, 0.0).astype(jnp.float32)
            value = whole[j, i * BW : (i + 1) * BW, :]
            mirror = whole[i, j * BW : (j + 1) * BW, :].T
            whole[j, i * BW : (i + 1) * BW, :] = value + share * (mirror - value)
    for owner in range(count):
        for i in range(touched):
            for j in range(touched):
                at = triangle(i) + j if j <= i else lower + triangle(j - 1) + i
                out[owner, at] = whole[j, pl.ds(i * BW + owner, each, stride=count), :]


def gram(coupling, weights, listed, count):
    depth, rows_all = coupling.shape
    touched = listed.shape[1]
    return pl.pallas_call(
        functools.partial(gram_kernel, touched=touched, count=count),
        out_shape=(
            jax.ShapeDtypeStruct((count, touched * touched, BW // count, BW), jnp.float32),
            jax.ShapeDtypeStruct((1, BW), jnp.int32),
        ),
        in_specs=[
            pl.BlockSpec(memory_space=pltpu.SMEM),
            pl.BlockSpec(memory_space=pl.ANY),
            pl.BlockSpec(memory_space=pltpu.VMEM),
        ],
        out_specs=(pl.BlockSpec(memory_space=pltpu.VMEM),) * 2,
        scratch_shapes=[
            pltpu.VMEM((depth, touched * BW), jnp.bfloat16),
            pltpu.VMEM((touched * BW, depth), jnp.bfloat16),
            pltpu.VMEM((touched, touched * BW, BW), jnp.float32),
            pltpu.SemaphoreType.DMA((touched,)),
        ],
        compiler_params=pltpu.CompilerParams(vmem_limit_bytes=50 * 1024 * 1024),
        name="gram",
    )(listed, coupling, weights)


def eliminate(tile, width=WIDTH):
    tiles = BW // 8
    sub = lax.broadcasted_iota(jnp.int32, (8, BW), 0)
    lane = lax.broadcasted_iota(jnp.int32, (8, BW), 1)
    a = [tile[8 * g : 8 * g + 8, :] for g in range(tiles)]
    v = [jnp.where(lane == sub + 8 * g, 1.0, 0.0).astype(jnp.float32) for g in range(tiles)]
    for j in range(0, BW, width):
        g0, s0 = j // 8, j % 8
        rows = [jnp.broadcast_to(a[g0][s0 + t : s0 + t + 1, :], (8, BW)) for t in range(width)]
        invs = [jnp.broadcast_to(v[g0][s0 + t : s0 + t + 1, :], (8, BW)) for t in range(width)]
        core = [
            [jnp.broadcast_to(rows[t][:, j + u : j + u + 1], (8, BW)) for u in range(width)] for t in range(width)
        ]
        ratios = []
        for t in range(width):
            recip = 1.0 / core[t][t]
            ratio = [core[t][u] * recip for u in range(width)]
            for u in range(t + 1, width):
                for w in range(u, width):
                    core[u][w] = core[u][w] - ratio[u] * core[t][w]
                rows[u] = rows[u] - ratio[u] * rows[t]
                invs[u] = invs[u] - ratio[u] * invs[t]
            ratios.append(ratio)
            rows[t], invs[t] = rows[t] * recip, invs[t] * recip
        for g in range(g0, tiles):
            own = [jnp.broadcast_to(a[g][:, j + t : j + t + 1], (8, BW)) for t in range(width)]
            for t in range(width):
                for u in range(t + 1, width):
                    own[u] = own[u] - own[t] * ratios[t][u]
            for t in range(width):
                use = jnp.where(sub > s0 + t, own[t], 0.0) if g == g0 else own[t]
                a[g] = a[g] - use * rows[t]
                v[g] = v[g] - use * invs[t]
    upper, inverse = [], []
    for g in range(tiles):
        own = jnp.sum(jnp.where(lane == sub + 8 * g, a[g], 0.0), axis=1, keepdims=True)
        scale = 1.0 / jnp.sqrt(own)
        upper.append(jnp.where(lane >= sub + 8 * g, a[g] * scale, 0.0))
        inverse.append(jnp.where(lane <= sub + 8 * g, v[g] * scale, 0.0))
    return jnp.concatenate(upper, axis=0).T, jnp.concatenate(inverse, axis=0)


def reversed_bits(value, bits):
    return sum(((value >> b) & 1) << (bits - 1 - b) for b in range(bits))


def send(source, target, sends, recvs, peer):
    return pltpu.make_async_remote_copy(
        src_ref=source,
        dst_ref=target,
        send_sem=sends,
        recv_sem=recvs,
        device_id={"scen": peer},
        device_id_type=MESH,
    )


def panel_kernel(pieces, table, diag, factor, trailing, *scratch, count, touched):
    (got, late, tabs, places, pan, bot, work, full, low, inverses, solved, *sems) = scratch
    early_s, early_r, tab_s, tab_r, late_s, late_r, pan_s, pan_r, bot_s, bot_r, own_sem = sems
    me = lax.axis_index("scen").astype(jnp.int32)
    bits = count.bit_length() - 1
    spot = sum(lax.rem(me // (1 << b), 2) * (1 << (bits - 1 - b)) for b in range(bits))
    each = BW // count
    panel = low.shape[1]
    steps = panel // BW
    blocks = diag.shape[1] // BW
    tail = trailing.shape[0]
    total = panel + tail
    lower, upper = triangle(touched), triangle(touched - 1)

    greet = pltpu.get_barrier_semaphore()

    def hello(m, carry):
        pl.semaphore_signal(greet, inc=1, device_id={"scen": lax.rem(me + m, count)}, device_id_type=MESH)
        return carry

    lax.fori_loop(1, count, hello, 0)
    pl.semaphore_wait(greet, count - 1)

    def early(m, to, at):
        return send(pieces.at[to, pl.ds(0, lower)], got.at[at, pl.ds(0, lower)], early_s.at[m], early_r.at[m], to)

    def tables(m, to, at):
        return send(table, tabs.at[at], tab_s.at[m], tab_r.at[m], to)

    def later(m, to, at):
        return send(pieces.at[to, pl.ds(lower, upper)], late.at[at, pl.ds(0, upper)], late_s.at[m], late_r.at[m], to)

    def start_early(m, carry):
        to = lax.rem(me + m, count)
        tables(m, to, me).start()
        early(m, to, me).start()
        return carry

    lax.fori_loop(1, count, start_early, 0)
    own_early = pltpu.make_async_copy(pieces.at[me, pl.ds(0, lower)], got.at[me, pl.ds(0, lower)], own_sem.at[0])
    own_late = pltpu.make_async_copy(pieces.at[me, pl.ds(lower, upper)], late.at[me, pl.ds(0, upper)], own_sem.at[1])
    own_early.start()
    own_late.start()
    tabs[me] = table[...]

    def blank(s, carry):
        got[s, lower:] = jnp.zeros((got.shape[1] - lower, each, BW), jnp.float32)
        late[s, upper:] = jnp.zeros((late.shape[1] - upper, each, BW), jnp.float32)
        return carry

    lax.fori_loop(0, count, blank, 0)
    low[...] = jnp.zeros_like(low)
    work[...] = jnp.zeros_like(work)
    own_early.wait()
    own_late.wait()

    def arrive_tables(m, carry):
        tables(m, lax.rem(me + m, count), me).wait_send()
        tables(m, lax.rem(me + m, count), lax.rem(me + count - m, count)).wait_recv()
        return carry

    lax.fori_loop(1, count, arrive_tables, 0)
    listing = pltpu.make_async_copy(tabs, places, own_sem.at[2])
    listing.start()
    listing.wait()

    def arrive_early(m, carry):
        early(m, lax.rem(me + m, count), me).wait_send()
        early(m, lax.rem(me + m, count), lax.rem(me + count - m, count)).wait_recv()
        return carry

    lax.fori_loop(1, count, arrive_early, 0)

    def gathered(source, row, row_at, column_at, columns):
        def add(s, sums):
            base = places[s, 0, row + row_at * blocks]
            return tuple(
                sums[k] + source[s, base + places[s, 0, columns[k] + column_at * blocks]]
                for k in range(len(columns))
            )

        sums = tuple(jnp.zeros((each, BW), jnp.float32) for _ in columns)
        batch = min(count, 16)

        def some(q, sums):
            for s in range(batch):
                sums = add(q * batch + s, sums)
            return sums

        return some(0, sums) if count == batch else lax.fori_loop(0, count // batch, some, sums)

    inner = lax.broadcasted_iota(jnp.int32, (each, BW), 0)
    lane = lax.broadcasted_iota(jnp.int32, (each, BW), 1)
    on_diag = lane == inner * count + me

    pan_first = [0]
    for j in range(steps):
        pan_first.append(pan_first[j] + count * (steps - j))
    bot_first = [count * steps * i for i in range(blocks - steps)]

    def relay(buf, first, width, sends, recvs, stage, chunk):
        span = 1 << stage
        mask = count >> (stage + 1)
        peer = me + mask - 2 * mask * lax.rem(me // mask, 2)
        at = pl.ds(first + (spot // span) * span * width, span * width)
        return send(buf.at[at], buf.at[at], sends.at[stage, chunk], recvs.at[stage, chunk], peer)

    def pan_relay(stage, j):
        return relay(pan, pan_first[j], steps - j, pan_s, pan_r, stage, j)

    def bot_relay(stage, i):
        return relay(bot, bot_first[i], steps, bot_s, bot_r, stage, i)

    def slot(make, chunks, t, done):
        for stage in range(bits, -1, -1):
            c = t - stage
            if 0 <= c < chunks:
                if stage > 0:
                    make(stage - 1, c).wait()
                if stage < bits:
                    make(stage, c).start()
                else:
                    done(c)

    def pan_done(j):
        for p in range(count):
            d = reversed_bits(p, bits)
            for t in range(steps - j):
                work[j, pl.ds((j + t) * BW + d, each, stride=count), :] = pan[
                    pan_first[j] + p * (steps - j) + t
                ]

    def bot_done(i):
        for p in range(count):
            d = reversed_bits(p, bits)
            for t in range(steps):
                full[t, pl.ds(i * BW + d, each, stride=count), :] = bot[bot_first[i] + p * steps + t]

    for i in range(steps):
        sums = gathered(got, i, 0, 1, range(i + 1))
        for j in range(i + 1):
            value = sums[j]
            if i == j:
                value = value + jnp.where(on_diag, diag[:, i * BW : (i + 1) * BW], 0.0)
            pan[pan_first[j] + spot * (steps - j) + i - j] = value
    pan_slots = steps + bits
    slot(pan_relay, steps, 0, pan_done)

    def bottom_row(i, carry):
        sums = gathered(got, steps + i, 0, 1, range(steps))
        at = pl.ds(pl.multiple_of(panel + i * each, each), each)
        for j in range(steps):
            bot[count * steps * i + spot * steps + j] = sums[j]
            work[j, at, :] = sums[j]
        return carry

    lax.fori_loop(0, blocks - steps, bottom_row, 0)
    for t in range(1, pan_slots):
        slot(pan_relay, steps, t, pan_done)

    def start_late(m, carry):
        later(m, lax.rem(me + m, count), me).start()
        return carry

    lax.fori_loop(1, count, start_late, 0)
    bot_slots = blocks - steps + bits
    share = -(-bot_slots // steps)

    def step(b, carry):
        for k in range(steps):

            @pl.when(b == k)
            def _():
                for t in range(k * share, min(bot_slots, (k + 1) * share)):
                    slot(bot_relay, blocks - steps, t, bot_done)

        place = pl.ds(pl.multiple_of(b * BW, BW), BW)
        left, inverse = eliminate(work[b, place, :])
        low[b, place, :] = left
        inverses[b] = inverse
        for k in range(steps):

            @pl.when(b == k)
            def _():
                lo, hi = k * BW, (k + 1) * BW
                strip = contract(work[k, hi:total, :], inverses[k], ((1,), (1,)))
                factor[tail:, lo:hi] = strip[panel - hi :]
                if hi < panel:
                    low[k, hi:panel, :] = strip[: panel - hi]
                    for at in range(hi, panel, BW * 2):
                        end = min(at + BW * 2, panel)
                        change = contract(strip[at - hi :], strip[at - hi : end - hi], ((1,), (1,)))
                        for q in range(at // BW, end // BW):
                            work[q, at:total, :] -= change[:, q * BW - at : (q + 1) * BW - at]

        return carry

    lax.fori_loop(0, steps, step, 0)
    for k in range(steps - 1, -1, -1):
        lo, hi = k * BW, (k + 1) * BW
        value = factor[tail:, lo:hi]
        if hi < panel:
            value = value - contract(solved[:, hi:panel], low[k, hi:panel, :], ((1,), (0,)))
        solved[:, lo:hi] = contract(value, inverses[k], ((1,), (0,)))
    for i in range(steps):
        for j in range(steps):
            factor[i * each : (i + 1) * each, j * BW : (j + 1) * BW] = low[
                j, pl.ds(i * BW + me, each, stride=count), :
            ]
    for at in range(0, trailing.shape[1], 2 * BW):
        right = jnp.concatenate([full[k, at : at + 2 * BW, :] for k in range(steps)], axis=1)
        trailing[:, at : at + 2 * BW] = -contract(solved[...], right, ((1,), (1,)))
    for i in range(blocks - steps):
        sums = gathered(got, steps + i, 0, 1, range(steps, steps + i + 1))
        for j in range(i + 1):
            value = sums[j]
            if i == j:
                value = value + jnp.where(on_diag, diag[:, (steps + i) * BW : (steps + i + 1) * BW], 0.0)
            trailing[i * each : (i + 1) * each, j * BW : (j + 1) * BW] += value

    def arrive_late(m, carry):
        later(m, lax.rem(me + m, count), me).wait_send()
        later(m, lax.rem(me + m, count), lax.rem(me + count - m, count)).wait_recv()
        return carry

    lax.fori_loop(1, count, arrive_late, 0)
    for i in range(blocks - steps):
        columns = range(steps + i + 1, blocks)
        if len(columns):
            sums = gathered(late, steps + i, 3, 2, columns)
            for k, j in enumerate(range(i + 1, blocks - steps)):
                trailing[i * each : (i + 1) * each, j * BW : (j + 1) * BW] += sums[k]


def panels(pieces, table, diag, touched):
    count, _, each, _ = pieces.shape
    rows_all = diag.shape[1]
    panel = rows_all // 2
    steps = panel // BW
    own = panel // count
    bits = count.bit_length() - 1
    dma = pltpu.SemaphoreType.DMA
    room = triangle(touched) + touched + 1 + triangle(touched) + 1
    late_room = triangle(touched - 1) + touched + triangle(touched - 1) + 1
    f32 = jnp.float32
    return pl.pallas_call(
        functools.partial(panel_kernel, count=count, touched=touched),
        out_shape=(
            jax.ShapeDtypeStruct((2 * own, panel), f32),
            jax.ShapeDtypeStruct((own, panel), f32),
        ),
        in_specs=[
            pl.BlockSpec(memory_space=pl.ANY),
            pl.BlockSpec(memory_space=pltpu.VMEM),
            pl.BlockSpec(memory_space=pltpu.VMEM),
        ],
        out_specs=(pl.BlockSpec(memory_space=pltpu.VMEM),) * 2,
        scratch_shapes=[
            pltpu.VMEM((count, room, each, BW), f32),
            pltpu.VMEM((count, late_room, each, BW), f32),
            pltpu.VMEM((count, 1, BW), jnp.int32),
            pltpu.SMEM((count, 1, BW), jnp.int32),
            pltpu.VMEM((count * triangle(steps), each, BW), f32),
            pltpu.VMEM((count * steps * steps, each, BW), f32),
            pltpu.VMEM((steps, panel + own, BW), f32),
            pltpu.VMEM((steps, panel, BW), f32),
            pltpu.VMEM((steps, panel, BW), f32),
            pltpu.VMEM((steps, BW, BW), f32),
            pltpu.VMEM((own, panel), f32),
        ]
        + [dma((count,))] * 6
        + [dma((bits, steps))] * 4
        + [dma((3,))],
        compiler_params=pltpu.CompilerParams(
            collective_id=0, has_side_effects=True, vmem_limit_bytes=56 * 1024 * 1024
        ),
        cost_estimate=pl.CostEstimate(flops=20_000_000_000, bytes_accessed=6_000_000, transcendentals=0),
        name="panels",
    )(pieces, table, diag)


def shards(scenario_rows, barrier, blocks, link_diag):
    count = lax.axis_size("scen")
    pieces, table = gram(scenario_rows[0], barrier, blocks, count)
    factor, trailing = panels(pieces, table, link_diag[None, :], blocks.shape[1])
    return (factor[:, None, :], trailing[:, None, :])


def solution(mesh):
    return jax.shard_map(
        shards,
        mesh=mesh,
        in_specs=(
            P(("group", "scen"), None, None),
            P(("group", "scen"), None),
            P(("group", "scen"), None),
            P("group"),
        ),
        out_specs=(P("group", "scen", None), P("group", "scen", None)),
        check_vma=False,
    )
```

```python
import functools

import jax
import jax.numpy as jnp
from jax import lax
from jax.experimental import pallas as pl
from jax.experimental.pallas import tpu as pltpu
from jax.sharding import PartitionSpec as P

BW = 128
WIDTH = 8
MESH = pl.DeviceIdType.MESH


def halves(value):
    high = value.astype(jnp.bfloat16)
    return high, (value - high.astype(jnp.float32)).astype(jnp.bfloat16)


def contract(left, right, dims):
    lh, ll = halves(left)
    rh, rl = halves(right)
    dot = functools.partial(
        lax.dot_general, dimension_numbers=(dims, ((), ())), preferred_element_type=jnp.float32
    )
    cross = dot(jnp.concatenate([lh, ll], axis=dims[0][0]), jnp.concatenate([rl, rh], axis=dims[1][0]))
    return dot(lh, rh) + cross


def triangle(n):
    return n * (n + 1) // 2


def gram_kernel(listed, coupling, weights, out, table, columns, lefts, whole, arrived, *, touched, count):
    depth, rows_all = coupling.shape
    each = BW // count
    blocks = rows_all // BW
    names = [listed[0, i] for i in range(touched)]
    for end in range(touched - 1, 0, -1):
        for i in range(end):
            names[i], names[i + 1] = jnp.minimum(names[i], names[i + 1]), jnp.maximum(names[i], names[i + 1])
    copies = []
    for i in range(touched):
        copy = pltpu.make_async_copy(
            coupling.at[:, pl.ds(pl.multiple_of(names[i] * BW, BW), BW)],
            columns.at[:, pl.ds(i * BW, BW)],
            arrived.at[i],
        )
        copy.start()
        copies.append(copy)
    lower, upper = triangle(touched), triangle(touched - 1)
    lane = lax.broadcasted_iota(jnp.int32, (1, BW), 1)
    index = jnp.where(lane < blocks, lower, jnp.where(lane < 2 * blocks, lower + touched + 1, 0))
    index = jnp.where((lane >= 2 * blocks) & (lane < 3 * blocks), upper, index)
    index = jnp.where((lane >= 3 * blocks) & (lane < 4 * blocks), upper + touched, index)
    for i in range(touched):
        index = jnp.where(lane == names[i], triangle(i), index)
        index = jnp.where(lane == names[i] + blocks, i, index)
        index = jnp.where(lane == names[i] + 2 * blocks, triangle(i - 1) if i else 0, index)
        index = jnp.where(lane == names[i] + 3 * blocks, i, index)
    table[...] = index
    dot = functools.partial(lax.dot_general, preferred_element_type=jnp.float32)
    pair = 2 if touched % 2 == 0 else 1
    for first in range(0, touched, pair):
        lo, hi = first * BW, (first + pair) * BW
        for i in range(first, first + pair):
            copies[i].wait()
        turned = columns[:, lo:hi].T
        lefts[lo:hi, :] = (weights[...] * turned.astype(jnp.float32)).astype(jnp.bfloat16)
        row = dot(lefts[lo:hi, :], columns[:, :hi], (((1,), (0,)), ((), ())))
        for j in range(first + pair):
            whole[j, lo:hi, :] = row[:, j * BW : (j + 1) * BW]
        if lo:
            column = dot(lefts[:lo, :], columns[:, lo:hi], (((1,), (0,)), ((), ())))
            for j in range(pair):
                whole[first + j, :lo, :] = column[:, j * BW : (j + 1) * BW]
    half = blocks // 4
    for i in range(touched):
        for j in range(i + 1):
            same = (names[i] // half == names[j] // half) & (names[i] < 2 * half)
            share = jnp.where(same, 0.5, 0.0).astype(jnp.float32)
            value = whole[j, i * BW : (i + 1) * BW, :]
            mirror = whole[i, j * BW : (j + 1) * BW, :].T
            whole[j, i * BW : (i + 1) * BW, :] = value + share * (mirror - value)
    for owner in range(count):
        for i in range(touched):
            for j in range(touched):
                at = triangle(i) + j if j <= i else lower + triangle(j - 1) + i
                out[owner, at] = whole[j, pl.ds(i * BW + owner, each, stride=count), :]


def gram(coupling, weights, listed, count):
    depth, rows_all = coupling.shape
    touched = listed.shape[1]
    return pl.pallas_call(
        functools.partial(gram_kernel, touched=touched, count=count),
        out_shape=(
            jax.ShapeDtypeStruct((count, touched * touched, BW // count, BW), jnp.float32),
            jax.ShapeDtypeStruct((1, BW), jnp.int32),
        ),
        in_specs=[
            pl.BlockSpec(memory_space=pltpu.SMEM),
            pl.BlockSpec(memory_space=pl.ANY),
            pl.BlockSpec(memory_space=pltpu.VMEM),
        ],
        out_specs=(pl.BlockSpec(memory_space=pltpu.VMEM),) * 2,
        scratch_shapes=[
            pltpu.VMEM((depth, touched * BW), jnp.bfloat16),
            pltpu.VMEM((touched * BW, depth), jnp.bfloat16),
            pltpu.VMEM((touched, touched * BW, BW), jnp.float32),
            pltpu.SemaphoreType.DMA((touched,)),
        ],
        compiler_params=pltpu.CompilerParams(vmem_limit_bytes=50 * 1024 * 1024),
        name="gram",
    )(listed, coupling, weights)


def eliminate(tile, width=WIDTH):
    tiles = BW // 8
    sub = lax.broadcasted_iota(jnp.int32, (8, BW), 0)
    lane = lax.broadcasted_iota(jnp.int32, (8, BW), 1)
    a = [tile[8 * g : 8 * g + 8, :] for g in range(tiles)]
    v = [jnp.where(lane == sub + 8 * g, 1.0, 0.0).astype(jnp.float32) for g in range(tiles)]
    for j in range(0, BW, width):
        g0, s0 = j // 8, j % 8
        rows = [jnp.broadcast_to(a[g0][s0 + t : s0 + t + 1, :], (8, BW)) for t in range(width)]
        invs = [jnp.broadcast_to(v[g0][s0 + t : s0 + t + 1, :], (8, BW)) for t in range(width)]
        core = [
            [jnp.broadcast_to(rows[t][:, j + u : j + u + 1], (8, BW)) for u in range(width)] for t in range(width)
        ]
        ratios = []
        for t in range(width):
            recip = 1.0 / core[t][t]
            ratio = [core[t][u] * recip for u in range(width)]
            for u in range(t + 1, width):
                for w in range(u, width):
                    core[u][w] = core[u][w] - ratio[u] * core[t][w]
                rows[u] = rows[u] - ratio[u] * rows[t]
                invs[u] = invs[u] - ratio[u] * invs[t]
            ratios.append(ratio)
            rows[t], invs[t] = rows[t] * recip, invs[t] * recip
        for g in range(g0, tiles):
            own = [jnp.broadcast_to(a[g][:, j + t : j + t + 1], (8, BW)) for t in range(width)]
            for t in range(width):
                for u in range(t + 1, width):
                    own[u] = own[u] - own[t] * ratios[t][u]
            for t in range(width):
                use = jnp.where(sub > s0 + t, own[t], 0.0) if g == g0 else own[t]
                a[g] = a[g] - use * rows[t]
                v[g] = v[g] - use * invs[t]
    upper, inverse = [], []
    for g in range(tiles):
        own = jnp.sum(jnp.where(lane == sub + 8 * g, a[g], 0.0), axis=1, keepdims=True)
        scale = 1.0 / jnp.sqrt(own)
        upper.append(jnp.where(lane >= sub + 8 * g, a[g] * scale, 0.0))
        inverse.append(jnp.where(lane <= sub + 8 * g, v[g] * scale, 0.0))
    return jnp.concatenate(upper, axis=0).T, jnp.concatenate(inverse, axis=0)


def reversed_bits(value, bits):
    return sum(((value >> b) & 1) << (bits - 1 - b) for b in range(bits))


def send(source, target, sends, recvs, peer):
    return pltpu.make_async_remote_copy(
        src_ref=source,
        dst_ref=target,
        send_sem=sends,
        recv_sem=recvs,
        device_id={"scen": peer},
        device_id_type=MESH,
    )


def panel_kernel(pieces, table, diag, factor, trailing, *scratch, count, touched):
    (got, late, tabs, places, pan, bot, work, full, low, highs, lows, inverses, solved, *sems) = scratch
    early_s, early_r, tab_s, tab_r, late_s, late_r, pan_s, pan_r, bot_s, bot_r, own_sem = sems
    me = lax.axis_index("scen").astype(jnp.int32)
    bits = count.bit_length() - 1
    spot = sum(lax.rem(me // (1 << b), 2) * (1 << (bits - 1 - b)) for b in range(bits))
    each = BW // count
    panel = low.shape[1]
    steps = panel // BW
    blocks = diag.shape[1] // BW
    tail = trailing.shape[0]
    total = work.shape[1]
    lower, upper = triangle(touched), triangle(touched - 1)

    greet = pltpu.get_barrier_semaphore()

    def hello(m, carry):
        pl.semaphore_signal(greet, inc=1, device_id={"scen": lax.rem(me + m, count)}, device_id_type=MESH)
        return carry

    lax.fori_loop(1, count, hello, 0)
    pl.semaphore_wait(greet, count - 1)

    def early(m, to, at):
        return send(pieces.at[to, pl.ds(0, lower)], got.at[at, pl.ds(0, lower)], early_s.at[m], early_r.at[m], to)

    def tables(m, to, at):
        return send(table, tabs.at[at], tab_s.at[m], tab_r.at[m], to)

    def later(m, to, at):
        return send(pieces.at[to, pl.ds(lower, upper)], late.at[at, pl.ds(0, upper)], late_s.at[m], late_r.at[m], to)

    def start_early(m, carry):
        to = lax.rem(me + m, count)
        tables(m, to, me).start()
        early(m, to, me).start()
        return carry

    lax.fori_loop(1, count, start_early, 0)
    own_early = pltpu.make_async_copy(pieces.at[me, pl.ds(0, lower)], got.at[me, pl.ds(0, lower)], own_sem.at[0])
    own_late = pltpu.make_async_copy(pieces.at[me, pl.ds(lower, upper)], late.at[me, pl.ds(0, upper)], own_sem.at[1])
    own_early.start()
    own_late.start()
    tabs[me] = table[...]

    def blank(s, carry):
        got[s, lower:] = jnp.zeros((got.shape[1] - lower, each, BW), jnp.float32)
        late[s, upper:] = jnp.zeros((late.shape[1] - upper, each, BW), jnp.float32)
        return carry

    lax.fori_loop(0, count, blank, 0)
    low[...] = jnp.zeros_like(low)
    work[...] = jnp.zeros_like(work)
    own_early.wait()
    own_late.wait()

    def arrive_tables(m, carry):
        tables(m, lax.rem(me + m, count), me).wait_send()
        tables(m, lax.rem(me + m, count), lax.rem(me + count - m, count)).wait_recv()
        return carry

    lax.fori_loop(1, count, arrive_tables, 0)
    listing = pltpu.make_async_copy(tabs, places, own_sem.at[2])
    listing.start()
    listing.wait()

    def arrive_early(m, carry):
        early(m, lax.rem(me + m, count), me).wait_send()
        early(m, lax.rem(me + m, count), lax.rem(me + count - m, count)).wait_recv()
        return carry

    lax.fori_loop(1, count, arrive_early, 0)

    def gathered(source, row, row_at, column_at, columns):
        def add(s, sums):
            base = places[s, 0, row + row_at * blocks]
            return tuple(
                sums[k] + source[s, base + places[s, 0, columns[k] + column_at * blocks]]
                for k in range(len(columns))
            )

        sums = tuple(jnp.zeros((each, BW), jnp.float32) for _ in columns)
        batch = min(count, 16)

        def some(q, sums):
            for s in range(batch):
                sums = add(q * batch + s, sums)
            return sums

        return some(0, sums) if count == batch else lax.fori_loop(0, count // batch, some, sums)

    inner = lax.broadcasted_iota(jnp.int32, (each, BW), 0)
    lane = lax.broadcasted_iota(jnp.int32, (each, BW), 1)
    on_diag = lane == inner * count + me

    pan_first = [0]
    for j in range(steps):
        pan_first.append(pan_first[j] + count * (steps - j))
    chunks = bot_s.shape[1]
    group = (blocks - steps) // chunks
    bot_first = [count * group * steps * c for c in range(chunks)]

    def relay(buf, first, width, sends, recvs, stage, chunk):
        span = 1 << stage
        mask = count >> (stage + 1)
        peer = me + mask - 2 * mask * lax.rem(me // mask, 2)
        at = pl.ds(first + (spot // span) * span * width, span * width)
        return send(buf.at[at], buf.at[at], sends.at[stage, chunk], recvs.at[stage, chunk], peer)

    def pan_relay(stage, j):
        return relay(pan, pan_first[j], steps - j, pan_s, pan_r, stage, j)

    def bot_relay(stage, i):
        return relay(bot, bot_first[i], group * steps, bot_s, bot_r, stage, i)

    def pan_slot(t):
        for stage in range(bits, -1, -1):
            c = t - stage
            if 0 <= c < steps:
                if stage > 0:
                    pan_relay(stage - 1, c).wait()
                if stage < bits:
                    pan_relay(stage, c).start()
                else:
                    pan_done(c)

    def bot_slot(t):
        for stage in range(bits, -1, -1):
            c = (t - 2 * stage) // 2 if stage == bits and (t - 2 * stage) % 2 == 0 else t - 2 * stage
            if stage == bits and (t - 2 * stage) % 2:
                continue
            if 0 <= c < chunks:
                if stage > 0:
                    bot_relay(stage - 1, c).wait()
                if stage < bits:
                    bot_relay(stage, c).start()
                else:
                    bot_done(c)

    def pan_done(j):
        for p in range(count):
            d = reversed_bits(p, bits)
            for t in range(steps - j):
                work[j, pl.ds((j + t) * BW + d, each, stride=count), :] = pan[
                    pan_first[j] + p * (steps - j) + t
                ]

    def bot_done(c):
        def piece(p, carry):
            d = sum(lax.rem(p // (1 << b), 2) * (1 << (bits - 1 - b)) for b in range(bits))
            for i in range(group):
                for t in range(steps):
                    full[t, pl.ds((c * group + i) * BW + d, each, stride=count), :] = bot[
                        bot_first[c] + (p * group + i) * steps + t
                    ]
            return carry

        lax.fori_loop(0, count, piece, 0)

    for i in range(steps):
        sums = gathered(got, i, 0, 1, range(i + 1))
        for j in range(i + 1):
            value = sums[j]
            if i == j:
                value = value + jnp.where(on_diag, diag[:, i * BW : (i + 1) * BW], 0.0)
            pan[pan_first[j] + spot * (steps - j) + i - j] = value
    pan_slot(0)

    def bottom_row(i, carry):
        sums = gathered(got, steps + i, 0, 1, range(steps))
        at = pl.ds(pl.multiple_of(panel + i * each, each), each)
        first = ((i // group) * count + spot) * group * steps + lax.rem(i, group) * steps
        for j in range(steps):
            bot[first + j] = sums[j]
            work[j, at, :] = sums[j]
        return carry

    lax.fori_loop(0, blocks - steps, bottom_row, 0)
    for t in range(1, bits + 1):
        pan_slot(t)

    def start_late(m, carry):
        later(m, lax.rem(me + m, count), me).start()
        return carry

    bot_slots = 2 * bits + 2 * (chunks - 1) + 1
    turns = 2 * steps
    late_turn = 2 + chunks

    def turn(t):
        if t < bot_slots:
            bot_slot(t)
        if t == late_turn:
            lax.fori_loop(1, count, start_late, 0)

    dot = functools.partial(lax.dot_general, preferred_element_type=jnp.float32)
    across = (((1,), (1,)), ((), ()))

    def step(b, carry):
        for k in range(steps):

            @pl.when(b == k)
            def _():
                lo, hi = k * BW, (k + 1) * BW
                if k:
                    pan_slot(k + bits)
                turn(2 * k)
                if k:
                    left_h = jnp.concatenate([highs[j, lo:total, :] for j in range(k)], axis=1)
                    left_l = jnp.concatenate([lows[j, lo:total, :] for j in range(k)], axis=1)
                    right_l = jnp.concatenate([lows[j, lo:hi, :] for j in range(k)], axis=1)
                    both = dot(left_h, jnp.concatenate([left_h[:BW], right_l], axis=0), across)
                    cross = dot(left_l, left_h[:BW], across)
                    work[k, lo:total, :] -= both[:, :BW] + (both[:, BW:] + cross)

        place = pl.ds(pl.multiple_of(b * BW, BW), BW)
        left, inverse = eliminate(work[b, place, :])
        low[b, place, :] = left
        inverses[b] = inverse
        for k in range(steps):

            @pl.when(b == k)
            def _():
                lo, hi = k * BW, (k + 1) * BW
                turn(2 * k + 1)
                strip = contract(work[k, hi:total, :], inverses[k], ((1,), (1,)))
                factor[tail:, lo:hi] = strip[panel - hi : panel - hi + tail]
                if hi < panel:
                    low[k, hi:panel, :] = strip[: panel - hi]
                    high, rest = halves(strip)
                    highs[k, hi:total, :] = high
                    lows[k, hi:total, :] = rest

        return carry

    lax.fori_loop(0, steps, step, 0)
    for t in range(turns, max(bot_slots, late_turn + 1)):
        turn(t)
    for k in range(steps - 1, -1, -1):
        lo, hi = k * BW, (k + 1) * BW
        value = factor[tail:, lo:hi]
        if hi < panel:
            sh, sl = halves(solved[:, hi:panel])
            down = (((1,), (0,)), ((), ()))
            high, rest = highs[k, hi:panel, :], lows[k, hi:panel, :]
            value = value - (dot(sh, high, down) + (dot(sh, rest, down) + dot(sl, high, down)))
        solved[:, lo:hi] = contract(value, inverses[k], ((1,), (0,)))
    for i in range(steps):
        for j in range(steps):
            factor[i * each : (i + 1) * each, j * BW : (j + 1) * BW] = low[
                j, pl.ds(i * BW + me, each, stride=count), :
            ]
    for at in range(0, trailing.shape[1], 2 * BW):
        right = jnp.concatenate([full[k, at : at + 2 * BW, :] for k in range(steps)], axis=1)
        trailing[:, at : at + 2 * BW] = -contract(solved[...], right, ((1,), (1,)))
    for i in range(blocks - steps):
        sums = gathered(got, steps + i, 0, 1, range(steps, steps + i + 1))
        for j in range(i + 1):
            value = sums[j]
            if i == j:
                value = value + jnp.where(on_diag, diag[:, (steps + i) * BW : (steps + i + 1) * BW], 0.0)
            trailing[i * each : (i + 1) * each, j * BW : (j + 1) * BW] += value

    def arrive_late(m, carry):
        later(m, lax.rem(me + m, count), me).wait_send()
        later(m, lax.rem(me + m, count), lax.rem(me + count - m, count)).wait_recv()
        return carry

    lax.fori_loop(1, count, arrive_late, 0)
    for i in range(blocks - steps):
        columns = range(steps + i + 1, blocks)
        if len(columns):
            sums = gathered(late, steps + i, 3, 2, columns)
            for k, j in enumerate(range(i + 1, blocks - steps)):
                trailing[i * each : (i + 1) * each, j * BW : (j + 1) * BW] += sums[k]


def panels(pieces, table, diag, touched):
    count, _, each, _ = pieces.shape
    rows_all = diag.shape[1]
    panel = rows_all // 2
    steps = panel // BW
    own = panel // count
    bits = count.bit_length() - 1
    rows = panel + -(-own // 16) * 16
    dma = pltpu.SemaphoreType.DMA
    room = triangle(touched) + touched + 1 + triangle(touched) + 1
    late_room = triangle(touched - 1) + touched + triangle(touched - 1) + 1
    f32 = jnp.float32
    return pl.pallas_call(
        functools.partial(panel_kernel, count=count, touched=touched),
        out_shape=(
            jax.ShapeDtypeStruct((2 * own, panel), f32),
            jax.ShapeDtypeStruct((own, panel), f32),
        ),
        in_specs=[
            pl.BlockSpec(memory_space=pl.ANY),
            pl.BlockSpec(memory_space=pltpu.VMEM),
            pl.BlockSpec(memory_space=pltpu.VMEM),
        ],
        out_specs=(pl.BlockSpec(memory_space=pltpu.VMEM),) * 2,
        scratch_shapes=[
            pltpu.VMEM((count, room, each, BW), f32),
            pltpu.VMEM((count, late_room, each, BW), f32),
            pltpu.VMEM((count, 1, BW), jnp.int32),
            pltpu.SMEM((count, 1, BW), jnp.int32),
            pltpu.VMEM((count * triangle(steps), each, BW), f32),
            pltpu.VMEM((count * steps * steps, each, BW), f32),
            pltpu.VMEM((steps, rows, BW), f32),
            pltpu.VMEM((steps, panel, BW), f32),
            pltpu.VMEM((steps, panel, BW), f32),
            pltpu.VMEM((steps, rows, BW), jnp.bfloat16),
            pltpu.VMEM((steps, rows, BW), jnp.bfloat16),
            pltpu.VMEM((steps, BW, BW), f32),
            pltpu.VMEM((own, panel), f32),
        ]
        + [dma((count,))] * 6
        + [dma((bits, steps))] * 2
        + [dma((bits, 4))] * 2
        + [dma((3,))],
        compiler_params=pltpu.CompilerParams(
            collective_id=0, has_side_effects=True, vmem_limit_bytes=56 * 1024 * 1024
        ),
        cost_estimate=pl.CostEstimate(flops=20_000_000_000, bytes_accessed=6_000_000, transcendentals=0),
        name="panels",
    )(pieces, table, diag)


def shards(scenario_rows, barrier, blocks, link_diag):
    count = lax.axis_size("scen")
    pieces, table = gram(scenario_rows[0], barrier, blocks, count)
    factor, trailing = panels(pieces, table, link_diag[None, :], blocks.shape[1])
    return (factor[:, None, :], trailing[:, None, :])


def solution(mesh):
    return jax.shard_map(
        shards,
        mesh=mesh,
        in_specs=(
            P(("group", "scen"), None, None),
            P(("group", "scen"), None),
            P(("group", "scen"), None),
            P("group"),
        ),
        out_specs=(P("group", "scen", None), P("group", "scen", None)),
        check_vma=False,
    )
```

```python
import functools

import jax
import jax.numpy as jnp
from jax import lax
from jax.experimental import pallas as pl
from jax.experimental.pallas import tpu as pltpu
from jax.sharding import PartitionSpec as P

BW = 128
WIDTH = 8
AHEAD = 4
MESH = pl.DeviceIdType.MESH


def halves(value):
    high = value.astype(jnp.bfloat16)
    return high, (value - high.astype(jnp.float32)).astype(jnp.bfloat16)


def contract(left, right, dims):
    lh, ll = halves(left)
    rh, rl = halves(right)
    dot = functools.partial(
        lax.dot_general, dimension_numbers=(dims, ((), ())), preferred_element_type=jnp.float32
    )
    cross = dot(jnp.concatenate([lh, ll], axis=dims[0][0]), jnp.concatenate([rl, rh], axis=dims[1][0]))
    return dot(lh, rh) + cross


def reversed_bits(value, bits):
    return sum(((value >> b) & 1) << (bits - 1 - b) for b in range(bits))


def triangle(n):
    return n * (n + 1) // 2


def gram_kernel(
    named, coupling, heavy, out, above, table, columns, lefts, whole, weights, listed, index, packed, uppers, arrived, left,
    *, touched, count,
):
    naming = pltpu.make_async_copy(named, listed, arrived.at[touched])
    weighing = pltpu.make_async_copy(heavy, weights, arrived.at[touched + 1])
    naming.start()
    weighing.start()
    naming.wait()
    depth, rows_all = coupling.shape
    each = BW // count
    blocks = rows_all // BW
    names = [listed[0, i] for i in range(touched)]
    for end in range(touched - 1, 0, -1):
        for i in range(end):
            names[i], names[i + 1] = jnp.minimum(names[i], names[i + 1]), jnp.maximum(names[i], names[i + 1])
    copies = []
    for i in range(touched):
        copy = pltpu.make_async_copy(
            coupling.at[:, pl.ds(pl.multiple_of(names[i] * BW, BW), BW)],
            columns.at[:, pl.ds(i * BW, BW)],
            arrived.at[i],
        )
        copy.start()
        copies.append(copy)
    lower = triangle(touched)
    lane = lax.broadcasted_iota(jnp.int32, (1, BW), 1)
    place = jnp.where(lane < blocks, lower, jnp.where(lane < 2 * blocks, lower + touched + 1, 0))
    for i in range(touched):
        place = jnp.where(lane == names[i], triangle(i), place)
        place = jnp.where(lane == names[i] + blocks, i, place)
    index[...] = place
    indexing = pltpu.make_async_copy(index, table, left.at[count])
    indexing.start()
    weighing.wait()
    dot = functools.partial(lax.dot_general, preferred_element_type=jnp.float32)
    pair = 2 if touched % 2 == 0 else 1
    for first in range(0, touched, pair):
        lo, hi = first * BW, (first + pair) * BW
        for i in range(first, first + pair):
            copies[i].wait()
        turned = columns[:, lo:hi].T
        lefts[lo:hi, :] = (weights[...] * turned.astype(jnp.float32)).astype(jnp.bfloat16)
        row = dot(lefts[lo:hi, :], columns[:, :hi], (((1,), (0,)), ((), ())))
        for j in range(first + pair):
            whole[j, lo:hi, :] = row[:, j * BW : (j + 1) * BW]
        if lo:
            column = dot(lefts[:lo, :], columns[:, lo:hi], (((1,), (0,)), ((), ())))
            for j in range(pair):
                whole[first + j, :lo, :] = column[:, j * BW : (j + 1) * BW]
    half = blocks // 4
    for i in range(touched):
        for j in range(i + 1):
            same = (names[i] // half == names[j] // half) & (names[i] < 2 * half)
            share = jnp.where(same, 0.5, 0.0).astype(jnp.float32)
            value = whole[j, i * BW : (i + 1) * BW, :]
            mirror = whole[i, j * BW : (j + 1) * BW, :].T
            whole[j, i * BW : (i + 1) * BW, :] = value + share * (mirror - value)
    for owner in range(count):
        for i in range(touched):
            for j in range(i + 1):
                packed[owner, triangle(i) + j] = whole[j, pl.ds(i * BW + owner, each, stride=count), :]
        pltpu.make_async_copy(packed.at[owner], out.at[owner], left.at[owner]).start()
    number = triangle(blocks // 2 - 1)
    uppers[...] = jnp.zeros_like(uppers)
    bits = count.bit_length() - 1
    for i in range(touched):
        for j in range(i + 1, touched):
            row, column = names[i] - blocks // 2, names[j] - blocks // 2

            @pl.when(row >= 0)
            def _():
                at = lax.div(column * (column - 1), 2) + row
                for owner in range(count):
                    first = reversed_bits(owner, bits) * number
                    uppers[first + at] = whole[j, pl.ds(i * BW + owner, each, stride=count), :]

    lifting = pltpu.make_async_copy(uppers, above, left.at[count + 1])
    lifting.start()
    lifting.wait()
    indexing.wait()
    for owner in range(count):
        pltpu.make_async_copy(packed.at[owner], out.at[owner], left.at[owner]).wait()


def gram(coupling, weights, listed, count):
    depth, rows_all = coupling.shape
    touched = listed.shape[1]
    number = triangle(rows_all // BW // 2 - 1)
    return pl.pallas_call(
        functools.partial(gram_kernel, touched=touched, count=count),
        out_shape=(
            jax.ShapeDtypeStruct((count, triangle(touched), BW // count, BW), jnp.float32),
            jax.ShapeDtypeStruct((count * number, BW // count, BW), jnp.float32),
            jax.ShapeDtypeStruct((1, BW), jnp.int32),
        ),
        in_specs=[
            pl.BlockSpec(memory_space=pltpu.HBM),
            pl.BlockSpec(memory_space=pltpu.HBM),
            pl.BlockSpec(memory_space=pltpu.HBM),
        ],
        out_specs=(pl.BlockSpec(memory_space=pltpu.HBM),) * 3,
        scratch_shapes=[
            pltpu.VMEM((depth, touched * BW), jnp.bfloat16),
            pltpu.VMEM((touched * BW, depth), jnp.bfloat16),
            pltpu.VMEM((touched, touched * BW, BW), jnp.float32),
            pltpu.VMEM((1, depth), jnp.float32),
            pltpu.SMEM((1, touched), jnp.int32),
            pltpu.VMEM((1, BW), jnp.int32),
            pltpu.VMEM((count, triangle(touched), BW // count, BW), jnp.float32),
            pltpu.VMEM((count * number, BW // count, BW), jnp.float32),
            pltpu.SemaphoreType.DMA((touched + 2,)),
            pltpu.SemaphoreType.DMA((count + 2,)),
        ],
        compiler_params=pltpu.CompilerParams(vmem_limit_bytes=60 * 1024 * 1024),
        name="gram",
    )(listed, coupling, weights)


def eliminate(tile, between, width=WIDTH):
    tiles = BW // 8
    sub = lax.broadcasted_iota(jnp.int32, (8, BW), 0)
    lane = lax.broadcasted_iota(jnp.int32, (8, BW), 1)
    a = [tile[8 * g : 8 * g + 8, :] for g in range(tiles)]
    v = [jnp.where(lane == sub + 8 * g, 1.0, 0.0).astype(jnp.float32) for g in range(tiles)]
    for j in range(0, BW, width):
        if j == BW // 2:
            between()
        g0, s0 = j // 8, j % 8
        rows = [jnp.broadcast_to(a[g0][s0 + t : s0 + t + 1, :], (8, BW)) for t in range(width)]
        invs = [jnp.broadcast_to(v[g0][s0 + t : s0 + t + 1, :], (8, BW)) for t in range(width)]
        core = [
            [jnp.broadcast_to(rows[t][:, j + u : j + u + 1], (8, BW)) for u in range(width)] for t in range(width)
        ]
        ratios = []
        for t in range(width):
            recip = 1.0 / core[t][t]
            ratio = [core[t][u] * recip for u in range(width)]
            for u in range(t + 1, width):
                for w in range(u, width):
                    core[u][w] = core[u][w] - ratio[u] * core[t][w]
                rows[u] = rows[u] - ratio[u] * rows[t]
                invs[u] = invs[u] - ratio[u] * invs[t]
            ratios.append(ratio)
            rows[t], invs[t] = rows[t] * recip, invs[t] * recip
        for g in range(g0, tiles):
            own = [jnp.broadcast_to(a[g][:, j + t : j + t + 1], (8, BW)) for t in range(width)]
            for t in range(width):
                for u in range(t + 1, width):
                    own[u] = own[u] - own[t] * ratios[t][u]
            for t in range(width):
                use = jnp.where(sub > s0 + t, own[t], 0.0) if g == g0 else own[t]
                a[g] = a[g] - use * rows[t]
                v[g] = v[g] - use * invs[t]
    upper, inverse = [], []
    for g in range(tiles):
        own = jnp.sum(jnp.where(lane == sub + 8 * g, a[g], 0.0), axis=1, keepdims=True)
        scale = 1.0 / jnp.sqrt(own)
        upper.append(jnp.where(lane >= sub + 8 * g, a[g] * scale, 0.0))
        inverse.append(jnp.where(lane <= sub + 8 * g, v[g] * scale, 0.0))
    return jnp.concatenate(upper, axis=0).T, jnp.concatenate(inverse, axis=0)


def send(source, target, sends, recvs, peer):
    return pltpu.make_async_remote_copy(
        src_ref=source,
        dst_ref=target,
        send_sem=sends,
        recv_sem=recvs,
        device_id={"scen": peer},
        device_id_type=MESH,
    )


def panel_kernel(pieces, above, table, diag, factor, trailing, *scratch, count, touched):
    (got, uppers, inbound, tabs, places, pan, bot, work, full, low, highs, lows, inverses, solved, trail, *sems) = scratch
    early_s, early_r, tab_s, tab_r, up_s, up_r, pan_s, pan_r, bot_s, bot_r, own_sem = sems
    me = lax.axis_index("scen").astype(jnp.int32)
    bits = count.bit_length() - 1
    spot = sum(lax.rem(me // (1 << b), 2) * (1 << (bits - 1 - b)) for b in range(bits))
    each = BW // count
    panel = low.shape[1]
    steps = panel // BW
    blocks = diag.shape[1] // BW
    tail = solved.shape[0]
    total = work.shape[1]
    lower = triangle(touched)
    number = triangle(blocks - steps - 1)

    greet = pltpu.get_barrier_semaphore()

    def hello(m, carry):
        pl.semaphore_signal(greet, inc=1, device_id={"scen": lax.rem(me + m, count)}, device_id_type=MESH)
        return carry

    lax.fori_loop(1, count, hello, 0)
    pl.semaphore_wait(greet, count - 1)

    def early(m, to, at):
        return send(pieces.at[to, pl.ds(0, lower)], got.at[at, pl.ds(0, lower)], early_s.at[m], early_r.at[m], to)

    def tables(m, to, at):
        return send(table, tabs.at[at], tab_s.at[m], tab_r.at[m], to)

    def lift(stage):
        size = count >> (stage + 1)
        mine = (spot // size) * size
        other = mine + size - 2 * size * lax.rem(spot // size, 2)
        mask = 1 << stage
        peer = me + mask - 2 * mask * lax.rem(me // mask, 2)
        source = uppers if stage else above
        first = count - 2 * size
        return send(
            source.at[pl.ds(other * number, size * number)],
            inbound.at[pl.ds(first * number, size * number)],
            up_s.at[stage],
            up_r.at[stage],
            peer,
        )

    def lifted(stage):
        size = count >> (stage + 1)
        mine = (spot // size) * size
        lift(stage).wait()

        def add(q, carry):
            to, by = pl.ds((mine + q) * number, number), pl.ds((count - 2 * size + q) * number, number)
            uppers[to] = uppers[to] + inbound[by]
            return carry

        lax.fori_loop(0, size, add, 0)
        if stage + 1 < bits:
            lift(stage + 1).start()

    def start_early(m, carry):
        to = lax.rem(me + m, count)
        tables(m, to, me).start()
        early(m, to, me).start()
        return carry

    lift(0).start()
    lax.fori_loop(1, count, start_early, 0)
    own_early = pltpu.make_async_copy(pieces.at[me, pl.ds(0, lower)], got.at[me, pl.ds(0, lower)], own_sem.at[0])
    kept = pl.ds((spot // (count // 2)) * (count // 2) * number, (count // 2) * number)
    own_late = pltpu.make_async_copy(above.at[kept], uppers.at[kept], own_sem.at[1])
    own_early.start()
    own_late.start()
    tabs[me] = table[...]

    def blank(s, carry):
        got[s, lower:] = jnp.zeros((got.shape[1] - lower, each, BW), jnp.float32)
        return carry

    lax.fori_loop(0, count, blank, 0)
    low[...] = jnp.zeros_like(low)
    work[...] = jnp.zeros_like(work)
    own_early.wait()
    own_late.wait()
    lifted(0)

    def arrive_tables(m, carry):
        tables(m, lax.rem(me + m, count), me).wait_send()
        tables(m, lax.rem(me + m, count), lax.rem(me + count - m, count)).wait_recv()
        return carry

    lax.fori_loop(1, count, arrive_tables, 0)
    listing = pltpu.make_async_copy(tabs, places, own_sem.at[2])
    listing.start()
    listing.wait()

    def arrive_early(m, carry):
        early(m, lax.rem(me + m, count), me).wait_send()
        early(m, lax.rem(me + m, count), lax.rem(me + count - m, count)).wait_recv()
        return carry

    lax.fori_loop(1, count, arrive_early, 0)

    def gathered(source, row, row_at, column_at, columns):
        def add(s, sums):
            base = places[s, 0, row + row_at * blocks]
            return tuple(
                sums[k] + source[s, base + places[s, 0, columns[k] + column_at * blocks]]
                for k in range(len(columns))
            )

        sums = tuple(jnp.zeros((each, BW), jnp.float32) for _ in columns)
        batch = min(count, 16)

        def some(q, sums):
            for s in range(batch):
                sums = add(q * batch + s, sums)
            return sums

        return some(0, sums) if count == batch else lax.fori_loop(0, count // batch, some, sums)

    inner = lax.broadcasted_iota(jnp.int32, (each, BW), 0)
    lane = lax.broadcasted_iota(jnp.int32, (each, BW), 1)
    on_diag = lane == inner * count + me

    pan_first = [0]
    for j in range(steps):
        pan_first.append(pan_first[j] + count * (steps - j))
    chunks = bot_s.shape[1]
    group = (blocks - steps) // chunks

    def relay(buf, first, width, sends, recvs, stage, chunk):
        span = 1 << stage
        mask = count >> (stage + 1)
        peer = me + mask - 2 * mask * lax.rem(me // mask, 2)
        at = pl.ds(first + (spot // span) * span * width, span * width)
        return send(buf.at[at], buf.at[at], sends.at[stage, chunk], recvs.at[stage, chunk], peer)

    def pan_relay(stage, j):
        return relay(pan, pan_first[j], steps - j, pan_s, pan_r, stage, j)

    def bot_relay(stage, i):
        return relay(bot, i * (count * group * steps), group * steps, bot_s, bot_r, stage, i)

    def pan_slot(t):
        for stage in range(bits, -1, -1):
            c = t - stage
            if 0 <= c < steps:
                if stage > 0:
                    pan_relay(stage - 1, c).wait()
                if stage < bits:
                    pan_relay(stage, c).start()
                else:
                    pan_done(c)

    def tick(t):
        for stage in range(bits):
            last = stage == bits - 1
            begin, period = (2 * bits + 2, 4) if last else (2 * stage, 3)
            ahead = jnp.maximum(t - begin, 0)
            pair = lax.div(ahead, period)

            @pl.when((t >= begin) & (lax.rem(ahead, period) == 0) & (pair < chunks // 2))
            def _():
                for c in (2 * pair, 2 * pair + 1):
                    if stage > 0:
                        bot_relay(stage - 1, c).wait()
                    bot_relay(stage, c).start()

            if last:

                @pl.when((t >= begin) & (lax.rem(ahead, period) == 0) & (pair > 0) & (pair < chunks // 2))
                def _():
                    for c in (2 * pair - 2, 2 * pair - 1):
                        bot_relay(stage, c).wait()
                        bot_done(c)

        @pl.when(t == 3 * bits)
        def _():
            for stage in range(2, bits - 1):
                lifted(stage)

    def pan_done(j):
        for p in range(count):
            d = reversed_bits(p, bits)
            for t in range(steps - j):
                work[j, pl.ds((j + t) * BW + d, each, stride=count), :] = pan[
                    pan_first[j] + p * (steps - j) + t
                ]

    def bot_done(c):
        def piece(p, carry):
            d = sum(lax.rem(p // (1 << b), 2) * (1 << (bits - 1 - b)) for b in range(bits))
            for i in range(group):
                for t in range(steps):
                    full[t, pl.ds((c * group + i) * BW + d, each, stride=count), :] = bot[
                        (c * count + p) * group * steps + i * steps + t
                    ]
            return carry

        lax.fori_loop(0, count, piece, 0)

    for i in range(steps):
        sums = gathered(got, i, 0, 1, range(i + 1))
        for j in range(i + 1):
            value = sums[j]
            if i == j:
                value = value + jnp.where(on_diag, diag[:, i * BW : (i + 1) * BW], 0.0)
            pan[pan_first[j] + spot * (steps - j) + i - j] = value
    pan_slot(0)
    lifted(1)

    def bottom_row(i, carry):
        sums = gathered(got, steps + i, 0, 1, range(steps))
        at = pl.ds(pl.multiple_of(panel + i * each, each), each)
        first = ((i // group) * count + spot) * group * steps + lax.rem(i, group) * steps
        for j in range(steps):
            bot[first + j] = sums[j]
            work[j, at, :] = sums[j]
        return carry

    lax.fori_loop(0, blocks - steps, bottom_row, 0)
    for t in range(1, bits):
        pan_slot(t)
        if t <= AHEAD:
            tick(t - 1)

    def corner_row(i, carry):
        sums = gathered(got, steps + i, 0, 1, range(steps, blocks))
        at = pl.ds(pl.multiple_of(i * each, each), each)
        for j in range(blocks - steps):
            own = jnp.where(on_diag & (i == j), diag[:, (steps + j) * BW : (steps + j + 1) * BW], 0.0)
            trail[j, at, :] = jnp.where(i >= j, sums[j], 0.0) + own
        return carry

    lax.fori_loop(0, blocks - steps, corner_row, 0)
    pan_slot(bits)
    for t in range(bits - 1, AHEAD):
        tick(t)

    dot = functools.partial(lax.dot_general, preferred_element_type=jnp.float32)
    across = (((1,), (1,)), ((), ()))

    def step(b, carry):
        for k in range(steps):

            @pl.when(b == k)
            def _():
                lo, hi = k * BW, (k + 1) * BW
                if k:
                    pan_slot(k + bits)
                    left_h = jnp.concatenate([highs[j, lo:total, :] for j in range(k)], axis=1)
                    left_l = jnp.concatenate([lows[j, lo:total, :] for j in range(k)], axis=1)
                    right_l = jnp.concatenate([lows[j, lo:hi, :] for j in range(k)], axis=1)
                    both = dot(left_h, jnp.concatenate([left_h[:BW], right_l], axis=0), across)
                    cross = dot(left_l, left_h[:BW], across)
                    work[k, lo:total, :] -= both[:, :BW] + (both[:, BW:] + cross)

        place = pl.ds(pl.multiple_of(b * BW, BW), BW)
        tick(AHEAD + 3 * b)
        left, inverse = eliminate(work[b, place, :], lambda: tick(AHEAD + 3 * b + 1))
        low[b, place, :] = left
        inverses[b] = inverse
        tick(AHEAD + 3 * b + 2)
        for k in range(steps):

            @pl.when(b == k)
            def _():
                lo, hi = k * BW, (k + 1) * BW
                strip = contract(work[k, hi:total, :], inverses[k], ((1,), (1,)))
                rest = strip[panel - hi : panel - hi + tail]
                solved[:, lo:hi] = rest
                factor[pl.ds(tail * steps + k, tail, stride=steps), :] = rest
                if hi < panel:
                    low[k, hi:panel, :] = strip[: panel - hi]
                    high, rest = halves(strip)
                    highs[k, hi:total, :] = high
                    lows[k, hi:total, :] = rest

        return carry

    lax.fori_loop(0, steps, step, 0)
    for k in range(steps - 1, -1, -1):
        lo, hi = k * BW, (k + 1) * BW
        value = solved[:, lo:hi]
        if hi < panel:
            sh, sl = halves(solved[:, hi:panel])
            down = (((1,), (0,)), ((), ()))
            high, rest = highs[k, hi:panel, :], lows[k, hi:panel, :]
            value = value - (dot(sh, high, down) + (dot(sh, rest, down) + dot(sl, high, down)))
        solved[:, lo:hi] = contract(value, inverses[k], ((1,), (0,)))
    for i in range(steps):
        for j in range(steps):
            factor[pl.ds(i * each * steps + j, each, stride=steps), :] = low[j, pl.ds(i * BW + me, each, stride=count), :]

    def extra(t, carry):
        tick(t)
        return carry

    lax.fori_loop(AHEAD + 3 * steps, 2 * bits + 2 + 4 * (chunks // 2 - 1) + 1, extra, 0)
    for c in range(chunks - 2, chunks):
        bot_relay(bits - 1, c).wait()
        bot_done(c)
    for at in range(0, panel, 2 * BW):
        right = jnp.concatenate([full[k, at : at + 2 * BW, :] for k in range(steps)], axis=1)
        change = contract(solved[...], right, ((1,), (1,)))
        for q in range(2):
            trail[at // BW + q] -= change[:, q * BW : (q + 1) * BW]

    lifted(bits - 1)
    for i in range(blocks - steps):
        for j in range(blocks - steps):
            value = trail[j, i * each : (i + 1) * each, :]
            if j > i:
                value = value + uppers[spot * number + triangle(j - 1) + i]
            trailing[pl.ds(i * each * steps + j, each, stride=steps), :] = value


def panels(pieces, above, table, diag, touched):
    count, _, each, _ = pieces.shape
    rows_all = diag.shape[1]
    panel = rows_all // 2
    steps = panel // BW
    own = panel // count
    bits = count.bit_length() - 1
    rows = panel + -(-own // 16) * 16
    dma = pltpu.SemaphoreType.DMA
    room = triangle(touched) + touched + 1 + triangle(touched) + 1
    blocks = rows_all // BW
    number = triangle(blocks - steps - 1)
    f32 = jnp.float32
    return pl.pallas_call(
        functools.partial(panel_kernel, count=count, touched=touched),
        out_shape=(
            jax.ShapeDtypeStruct((2 * own * steps, BW), f32),
            jax.ShapeDtypeStruct((own * steps, BW), f32),
        ),
        in_specs=[
            pl.BlockSpec(memory_space=pltpu.HBM),
            pl.BlockSpec(memory_space=pltpu.HBM),
            pl.BlockSpec(memory_space=pltpu.VMEM),
            pl.BlockSpec(memory_space=pltpu.VMEM),
        ],
        out_specs=(pl.BlockSpec(memory_space=pltpu.VMEM),) * 2,
        scratch_shapes=[
            pltpu.VMEM((count, room, each, BW), f32),
            pltpu.VMEM((count * number, each, BW), f32),
            pltpu.VMEM(((count - 1) * number, each, BW), f32),
            pltpu.VMEM((count, 1, BW), jnp.int32),
            pltpu.SMEM((count, 1, BW), jnp.int32),
            pltpu.VMEM((count * triangle(steps), each, BW), f32),
            pltpu.VMEM((count * steps * steps, each, BW), f32),
            pltpu.VMEM((steps, rows, BW), f32),
            pltpu.VMEM((steps, panel, BW), f32),
            pltpu.VMEM((steps, panel, BW), f32),
            pltpu.VMEM((steps, rows, BW), jnp.bfloat16),
            pltpu.VMEM((steps, rows, BW), jnp.bfloat16),
            pltpu.VMEM((steps, BW, BW), f32),
            pltpu.VMEM((own, panel), f32),
            pltpu.VMEM((blocks - steps, own, BW), f32),
        ]
        + [dma((count,))] * 4
        + [dma((bits,))] * 2
        + [dma((bits, steps))] * 2
        + [dma((bits, 8))] * 2
        + [dma((3,))],
        compiler_params=pltpu.CompilerParams(
            collective_id=0, has_side_effects=True, vmem_limit_bytes=60 * 1024 * 1024
        ),
        cost_estimate=pl.CostEstimate(flops=20_000_000_000, bytes_accessed=6_000_000, transcendentals=0),
        name="panels",
    )(pieces, above, table, diag)


def hand_kernel(factor, trailing, factor_out, trailing_out, done):
    copies = [
        pltpu.make_async_copy(factor, factor_out, done.at[0]),
        pltpu.make_async_copy(trailing, trailing_out, done.at[1]),
    ]
    for copy in copies:
        copy.start()
    for copy in copies:
        copy.wait()


def hand(factor, trailing):
    return pl.pallas_call(
        hand_kernel,
        out_shape=tuple(jax.ShapeDtypeStruct(a.shape, a.dtype) for a in (factor, trailing)),
        in_specs=[pl.BlockSpec(memory_space=pltpu.VMEM)] * 2,
        out_specs=(pl.BlockSpec(memory_space=pltpu.HBM),) * 2,
        scratch_shapes=[pltpu.SemaphoreType.DMA((2,))],
        name="hand",
    )(factor, trailing)


def shards(scenario_rows, barrier, blocks, link_diag):
    count = lax.axis_size("scen")
    pieces, above, table = gram(scenario_rows[0], barrier, blocks, count)
    factor, trailing = panels(pieces, above, table, link_diag[None, :], blocks.shape[1])
    factor, trailing = hand(factor, trailing)
    panel = link_diag.shape[0] // 2
    return (factor.reshape(-1, 1, panel), trailing.reshape(-1, 1, panel))


def solution(mesh):
    return jax.shard_map(
        shards,
        mesh=mesh,
        in_specs=(
            P(("group", "scen"), None, None),
            P(("group", "scen"), None),
            P(("group", "scen"), None),
            P("group"),
        ),
        out_specs=(P("group", "scen", None), P("group", "scen", None)),
        check_vma=False,
    )
```

```python
import functools

import jax
import jax.numpy as jnp
from jax import lax
from jax.experimental import pallas as pl
from jax.experimental.pallas import tpu as pltpu
from jax.sharding import PartitionSpec as P

BW = 128
WIDTH = 8
AHEAD = 2
MESH = pl.DeviceIdType.MESH


def halves(value):
    high = value.astype(jnp.bfloat16)
    return high, (value - high.astype(jnp.float32)).astype(jnp.bfloat16)


def contract(left, right, dims):
    lh, ll = halves(left)
    rh, rl = halves(right)
    dot = functools.partial(
        lax.dot_general, dimension_numbers=(dims, ((), ())), preferred_element_type=jnp.float32
    )
    cross = dot(jnp.concatenate([lh, ll], axis=dims[0][0]), jnp.concatenate([rl, rh], axis=dims[1][0]))
    return dot(lh, rh) + cross


def reversed_bits(value, bits):
    return sum(((value >> b) & 1) << (bits - 1 - b) for b in range(bits))


def triangle(n):
    return n * (n + 1) // 2


def gram_kernel(
    named, coupling, heavy, out, above, table, columns, lefts, whole, weights, listed, index, packed, uppers, arrived, left,
    *, touched, count,
):
    naming = pltpu.make_async_copy(named, listed, arrived.at[touched])
    weighing = pltpu.make_async_copy(heavy, weights, arrived.at[touched + 1])
    naming.start()
    weighing.start()
    naming.wait()
    depth, rows_all = coupling.shape
    each = BW // count
    blocks = rows_all // BW
    names = [listed[0, i] for i in range(touched)]
    for end in range(touched - 1, 0, -1):
        for i in range(end):
            names[i], names[i + 1] = jnp.minimum(names[i], names[i + 1]), jnp.maximum(names[i], names[i + 1])
    copies = []
    for i in range(touched):
        copy = pltpu.make_async_copy(
            coupling.at[:, pl.ds(pl.multiple_of(names[i] * BW, BW), BW)],
            columns.at[:, pl.ds(i * BW, BW)],
            arrived.at[i],
        )
        copy.start()
        copies.append(copy)
    lower = triangle(touched)
    lane = lax.broadcasted_iota(jnp.int32, (1, BW), 1)
    place = jnp.where(lane < blocks, lower, jnp.where(lane < 2 * blocks, lower + touched + 1, 0))
    for i in range(touched):
        place = jnp.where(lane == names[i], triangle(i), place)
        place = jnp.where(lane == names[i] + blocks, i, place)
    index[...] = place
    indexing = pltpu.make_async_copy(index, table, left.at[count])
    indexing.start()
    weighing.wait()
    dot = functools.partial(lax.dot_general, preferred_element_type=jnp.float32)
    pair = 2 if touched % 2 == 0 else 1
    for first in range(0, touched, pair):
        lo, hi = first * BW, (first + pair) * BW
        for i in range(first, first + pair):
            copies[i].wait()
        turned = columns[:, lo:hi].T
        lefts[lo:hi, :] = (weights[...] * turned.astype(jnp.float32)).astype(jnp.bfloat16)
        row = dot(lefts[lo:hi, :], columns[:, :hi], (((1,), (0,)), ((), ())))
        for j in range(first + pair):
            whole[j, lo:hi, :] = row[:, j * BW : (j + 1) * BW]
        if lo:
            column = dot(lefts[:lo, :], columns[:, lo:hi], (((1,), (0,)), ((), ())))
            for j in range(pair):
                whole[first + j, :lo, :] = column[:, j * BW : (j + 1) * BW]
    half = blocks // 4
    for i in range(touched):
        for j in range(i + 1):
            same = (names[i] // half == names[j] // half) & (names[i] < 2 * half)
            share = jnp.where(same, 0.5, 0.0).astype(jnp.float32)
            value = whole[j, i * BW : (i + 1) * BW, :]
            mirror = whole[i, j * BW : (j + 1) * BW, :].T
            whole[j, i * BW : (i + 1) * BW, :] = value + share * (mirror - value)
    number = triangle(blocks // 2 - 1)
    uppers[...] = jnp.zeros_like(uppers)
    bits = count.bit_length() - 1
    for i in range(touched):
        for j in range(i + 1, touched):
            row, column = names[i] - blocks // 2, names[j] - blocks // 2

            @pl.when(row >= 0)
            def _():
                at = lax.div(column * (column - 1), 2) + row
                for owner in range(count):
                    first = reversed_bits(owner, bits) * number
                    uppers[first + at] = whole[j, pl.ds(i * BW + owner, each, stride=count), :]

    lifting = pltpu.make_async_copy(uppers, above, left.at[count + 1])
    lifting.start()
    for owner in range(count):
        for i in range(touched):
            for j in range(i + 1):
                packed[owner, triangle(i) + j] = whole[j, pl.ds(i * BW + owner, each, stride=count), :]
        pltpu.make_async_copy(packed.at[owner], out.at[owner], left.at[owner]).start()
    lifting.wait()
    indexing.wait()
    for owner in range(count):
        pltpu.make_async_copy(packed.at[owner], out.at[owner], left.at[owner]).wait()


def gram(coupling, weights, listed, count):
    depth, rows_all = coupling.shape
    touched = listed.shape[1]
    number = triangle(rows_all // BW // 2 - 1)
    return pl.pallas_call(
        functools.partial(gram_kernel, touched=touched, count=count),
        out_shape=(
            jax.ShapeDtypeStruct((count, triangle(touched), BW // count, BW), jnp.float32),
            jax.ShapeDtypeStruct((count * number, BW // count, BW), jnp.float32),
            jax.ShapeDtypeStruct((1, BW), jnp.int32),
        ),
        in_specs=[
            pl.BlockSpec(memory_space=pltpu.HBM),
            pl.BlockSpec(memory_space=pltpu.HBM),
            pl.BlockSpec(memory_space=pltpu.HBM),
        ],
        out_specs=(pl.BlockSpec(memory_space=pltpu.HBM),) * 3,
        scratch_shapes=[
            pltpu.VMEM((depth, touched * BW), jnp.bfloat16),
            pltpu.VMEM((touched * BW, depth), jnp.bfloat16),
            pltpu.VMEM((touched, touched * BW, BW), jnp.float32),
            pltpu.VMEM((1, depth), jnp.float32),
            pltpu.SMEM((1, touched), jnp.int32),
            pltpu.VMEM((1, BW), jnp.int32),
            pltpu.VMEM((count, triangle(touched), BW // count, BW), jnp.float32),
            pltpu.VMEM((count * number, BW // count, BW), jnp.float32),
            pltpu.SemaphoreType.DMA((touched + 2,)),
            pltpu.SemaphoreType.DMA((count + 2,)),
        ],
        compiler_params=pltpu.CompilerParams(vmem_limit_bytes=60 * 1024 * 1024),
        name="gram",
    )(listed, coupling, weights)


def eliminate(tile, between, width=WIDTH):
    tiles = BW // 8
    sub = lax.broadcasted_iota(jnp.int32, (8, BW), 0)
    lane = lax.broadcasted_iota(jnp.int32, (8, BW), 1)
    a = [tile[8 * g : 8 * g + 8, :] for g in range(tiles)]
    v = [jnp.where(lane == sub + 8 * g, 1.0, 0.0).astype(jnp.float32) for g in range(tiles)]
    for j in range(0, BW, width):
        if j == BW // 2:
            between()
        g0, s0 = j // 8, j % 8
        rows = [jnp.broadcast_to(a[g0][s0 + t : s0 + t + 1, :], (8, BW)) for t in range(width)]
        invs = [jnp.broadcast_to(v[g0][s0 + t : s0 + t + 1, :], (8, BW)) for t in range(width)]
        core = [
            [jnp.broadcast_to(rows[t][:, j + u : j + u + 1], (8, BW)) for u in range(width)] for t in range(width)
        ]
        ratios = []
        for t in range(width):
            recip = 1.0 / core[t][t]
            ratio = [core[t][u] * recip for u in range(width)]
            for u in range(t + 1, width):
                for w in range(u, width):
                    core[u][w] = core[u][w] - ratio[u] * core[t][w]
                rows[u] = rows[u] - ratio[u] * rows[t]
                invs[u] = invs[u] - ratio[u] * invs[t]
            ratios.append(ratio)
            rows[t], invs[t] = rows[t] * recip, invs[t] * recip
        for g in range(g0, tiles):
            own = [jnp.broadcast_to(a[g][:, j + t : j + t + 1], (8, BW)) for t in range(width)]
            for t in range(width):
                for u in range(t + 1, width):
                    own[u] = own[u] - own[t] * ratios[t][u]
            for t in range(width):
                use = jnp.where(sub > s0 + t, own[t], 0.0) if g == g0 else own[t]
                a[g] = a[g] - use * rows[t]
                v[g] = v[g] - use * invs[t]
    upper, inverse = [], []
    for g in range(tiles):
        own = jnp.sum(jnp.where(lane == sub + 8 * g, a[g], 0.0), axis=1, keepdims=True)
        scale = 1.0 / jnp.sqrt(own)
        upper.append(jnp.where(lane >= sub + 8 * g, a[g] * scale, 0.0))
        inverse.append(jnp.where(lane <= sub + 8 * g, v[g] * scale, 0.0))
    return jnp.concatenate(upper, axis=0).T, jnp.concatenate(inverse, axis=0)


def send(source, target, sends, recvs, peer):
    return pltpu.make_async_remote_copy(
        src_ref=source,
        dst_ref=target,
        send_sem=sends,
        recv_sem=recvs,
        device_id={"scen": peer},
        device_id_type=MESH,
    )


def panel_kernel(pieces, above, table, diag, factor, trailing, *scratch, count, touched):
    (got, uppers, inbound, tabs, places, pan, bot, work, full, low, highs, lows, inverses, solved, trail, *sems) = scratch
    early_s, early_r, tab_s, tab_r, up_s, up_r, pan_s, pan_r, bot_s, bot_r, own_sem = sems
    me = lax.axis_index("scen").astype(jnp.int32)
    bits = count.bit_length() - 1
    spot = sum(lax.rem(me // (1 << b), 2) * (1 << (bits - 1 - b)) for b in range(bits))
    each = BW // count
    panel = low.shape[1]
    steps = panel // BW
    blocks = diag.shape[1] // BW
    tail = solved.shape[0]
    total = work.shape[1]
    lower = triangle(touched)
    number = triangle(blocks - steps - 1)

    greet = pltpu.get_barrier_semaphore()

    def hello(m, carry):
        pl.semaphore_signal(greet, inc=1, device_id={"scen": lax.rem(me + m, count)}, device_id_type=MESH)
        return carry

    lax.fori_loop(1, count, hello, 0)
    pl.semaphore_wait(greet, count - 1)

    def early(m, to, at):
        return send(pieces.at[to, pl.ds(0, lower)], got.at[at, pl.ds(0, lower)], early_s.at[m], early_r.at[m], to)

    def tables(m, to, at):
        return send(table, tabs.at[at], tab_s.at[m], tab_r.at[m], to)

    def lift(stage):
        size = count >> (stage + 1)
        mine = (spot // size) * size
        other = mine + size - 2 * size * lax.rem(spot // size, 2)
        mask = 1 << stage
        peer = me + mask - 2 * mask * lax.rem(me // mask, 2)
        source = uppers if stage else above
        first = count - 2 * size
        return send(
            source.at[pl.ds(other * number, size * number)],
            inbound.at[pl.ds(first * number, size * number)],
            up_s.at[stage],
            up_r.at[stage],
            peer,
        )

    def lifted(stage):
        size = count >> (stage + 1)
        mine = (spot // size) * size
        lift(stage).wait()

        def add(q, carry):
            to, by = pl.ds((mine + q) * number, number), pl.ds((count - 2 * size + q) * number, number)
            uppers[to] = uppers[to] + inbound[by]
            return carry

        lax.fori_loop(0, size, add, 0)
        if stage + 1 < bits:
            lift(stage + 1).start()

    def start_early(m, carry):
        to = lax.rem(me + m, count)
        tables(m, to, me).start()
        early(m, to, me).start()
        return carry

    lift(0).start()
    lax.fori_loop(1, count, start_early, 0)
    own_early = pltpu.make_async_copy(pieces.at[me, pl.ds(0, lower)], got.at[me, pl.ds(0, lower)], own_sem.at[0])
    kept = pl.ds((spot // (count // 2)) * (count // 2) * number, (count // 2) * number)
    own_late = pltpu.make_async_copy(above.at[kept], uppers.at[kept], own_sem.at[1])
    own_early.start()
    own_late.start()
    tabs[me] = table[...]

    def blank(s, carry):
        got[s, lower:] = jnp.zeros((got.shape[1] - lower, each, BW), jnp.float32)
        return carry

    lax.fori_loop(0, count, blank, 0)
    low[...] = jnp.zeros_like(low)
    work[...] = jnp.zeros_like(work)
    own_early.wait()
    own_late.wait()
    lifted(0)

    def arrive_tables(m, carry):
        tables(m, lax.rem(me + m, count), me).wait_send()
        tables(m, lax.rem(me + m, count), lax.rem(me + count - m, count)).wait_recv()
        return carry

    lax.fori_loop(1, count, arrive_tables, 0)
    listing = pltpu.make_async_copy(tabs, places, own_sem.at[2])
    listing.start()
    listing.wait()

    def arrive_early(m, carry):
        early(m, lax.rem(me + m, count), me).wait_send()
        early(m, lax.rem(me + m, count), lax.rem(me + count - m, count)).wait_recv()
        return carry

    lax.fori_loop(1, count, arrive_early, 0)

    def gathered(source, row, row_at, column_at, columns):
        def add(s, sums):
            base = places[s, 0, row + row_at * blocks]
            return tuple(
                sums[k] + source[s, base + places[s, 0, columns[k] + column_at * blocks]]
                for k in range(len(columns))
            )

        sums = tuple(jnp.zeros((each, BW), jnp.float32) for _ in columns)
        batch = min(count, 16)

        def some(q, sums):
            for s in range(batch):
                sums = add(q * batch + s, sums)
            return sums

        return some(0, sums) if count == batch else lax.fori_loop(0, count // batch, some, sums)

    inner = lax.broadcasted_iota(jnp.int32, (each, BW), 0)
    lane = lax.broadcasted_iota(jnp.int32, (each, BW), 1)
    on_diag = lane == inner * count + me

    pan_first = [0]
    for j in range(steps):
        pan_first.append(pan_first[j] + count * (steps - j))
    chunks = bot_s.shape[1]
    group = (blocks - steps) // chunks

    def relay(buf, first, width, sends, recvs, stage, chunk):
        span = 1 << stage
        mask = count >> (stage + 1)
        peer = me + mask - 2 * mask * lax.rem(me // mask, 2)
        at = pl.ds(first + (spot // span) * span * width, span * width)
        return send(buf.at[at], buf.at[at], sends.at[stage, chunk], recvs.at[stage, chunk], peer)

    def pan_relay(stage, j):
        return relay(pan, pan_first[j], steps - j, pan_s, pan_r, stage, j)

    def bot_relay(stage, i):
        return relay(bot, i * (count * group * steps), group * steps, bot_s, bot_r, stage, i)

    def pan_slot(t):
        for stage in range(bits, -1, -1):
            c = t - stage
            if 0 <= c < steps:
                if stage > 0:
                    pan_relay(stage - 1, c).wait()
                if stage < bits:
                    pan_relay(stage, c).start()
                else:
                    pan_done(c)

    def tick(t):
        for stage in range(bits):
            last = stage == bits - 1
            begin, period = (2 * bits + 2, 4) if last else (2 * stage, 3)
            ahead = jnp.maximum(t - begin, 0)
            pair = lax.div(ahead, period)

            @pl.when((t >= begin) & (lax.rem(ahead, period) == 0) & (pair < chunks // 2))
            def _():
                for c in (2 * pair, 2 * pair + 1):
                    if stage > 0:
                        bot_relay(stage - 1, c).wait()
                    bot_relay(stage, c).start()

            if last:

                @pl.when((t >= begin) & (lax.rem(ahead, period) == 0) & (pair > 0) & (pair < chunks // 2))
                def _():
                    for c in (2 * pair - 2, 2 * pair - 1):
                        bot_relay(stage, c).wait()
                        bot_done(c)

        @pl.when(t == 3 * bits)
        def _():
            for stage in range(2, bits - 1):
                lifted(stage)

    def pan_done(j):
        for p in range(count):
            d = reversed_bits(p, bits)
            for t in range(steps - j):
                work[j, pl.ds((j + t) * BW + d, each, stride=count), :] = pan[
                    pan_first[j] + p * (steps - j) + t
                ]

    def bot_done(c):
        def piece(p, carry):
            d = sum(lax.rem(p // (1 << b), 2) * (1 << (bits - 1 - b)) for b in range(bits))
            for i in range(group):
                for t in range(steps):
                    full[t, pl.ds((c * group + i) * BW + d, each, stride=count), :] = bot[
                        (c * count + p) * group * steps + i * steps + t
                    ]
            return carry

        lax.fori_loop(0, count, piece, 0)

    for i in range(steps):
        sums = gathered(got, i, 0, 1, range(i + 1))
        for j in range(i + 1):
            value = sums[j]
            if i == j:
                value = value + jnp.where(on_diag, diag[:, i * BW : (i + 1) * BW], 0.0)
            pan[pan_first[j] + spot * (steps - j) + i - j] = value
    pan_slot(0)
    lifted(1)

    def bottom_row(i, carry):
        sums = gathered(got, steps + i, 0, 1, range(steps))
        at = pl.ds(pl.multiple_of(panel + i * each, each), each)
        first = ((i // group) * count + spot) * group * steps + lax.rem(i, group) * steps
        for j in range(steps):
            bot[first + j] = sums[j]
            work[j, at, :] = sums[j]
        return carry

    lax.fori_loop(0, blocks - steps, bottom_row, 0)
    for t in range(1, bits):
        pan_slot(t)
        if t <= AHEAD:
            tick(t - 1)

    def corner_row(i, carry):
        sums = gathered(got, steps + i, 0, 1, range(steps, blocks))
        at = pl.ds(pl.multiple_of(i * each, each), each)
        for j in range(blocks - steps):
            own = jnp.where(on_diag & (i == j), diag[:, (steps + j) * BW : (steps + j + 1) * BW], 0.0)
            trail[j, at, :] = jnp.where(i >= j, sums[j], 0.0) + own
        return carry

    lax.fori_loop(0, blocks - steps, corner_row, 0)
    pan_slot(bits)
    for t in range(bits - 1, AHEAD):
        tick(t)

    dot = functools.partial(lax.dot_general, preferred_element_type=jnp.float32)
    across = (((1,), (1,)), ((), ()))

    def step(b, carry):
        for k in range(steps):

            @pl.when(b == k)
            def _():
                lo, hi = k * BW, (k + 1) * BW
                if k:
                    pan_slot(k + bits)
                    left_h = jnp.concatenate([highs[j, lo:total, :] for j in range(k)], axis=1)
                    left_l = jnp.concatenate([lows[j, lo:total, :] for j in range(k)], axis=1)
                    right_l = jnp.concatenate([lows[j, lo:hi, :] for j in range(k)], axis=1)
                    both = dot(left_h, jnp.concatenate([left_h[:BW], right_l], axis=0), across)
                    cross = dot(left_l, left_h[:BW], across)
                    work[k, lo:total, :] -= both[:, :BW] + (both[:, BW:] + cross)

        place = pl.ds(pl.multiple_of(b * BW, BW), BW)
        tick(AHEAD + 3 * b)
        left, inverse = eliminate(work[b, place, :], lambda: tick(AHEAD + 3 * b + 1))
        low[b, place, :] = left
        inverses[b] = inverse
        tick(AHEAD + 3 * b + 2)
        for k in range(steps):

            @pl.when(b == k)
            def _():
                lo, hi = k * BW, (k + 1) * BW
                strip = contract(work[k, hi:total, :], inverses[k], ((1,), (1,)))
                rest = strip[panel - hi : panel - hi + tail]
                solved[:, lo:hi] = rest
                factor[pl.ds(tail * steps + k, tail, stride=steps), :] = rest
                if hi < panel:
                    low[k, hi:panel, :] = strip[: panel - hi]
                    high, rest = halves(strip)
                    highs[k, hi:total, :] = high
                    lows[k, hi:total, :] = rest

        return carry

    lax.fori_loop(0, steps, step, 0)
    for k in range(steps - 1, -1, -1):
        lo, hi = k * BW, (k + 1) * BW
        value = solved[:, lo:hi]
        if hi < panel:
            sh, sl = halves(solved[:, hi:panel])
            down = (((1,), (0,)), ((), ()))
            high, rest = highs[k, hi:panel, :], lows[k, hi:panel, :]
            value = value - (dot(sh, high, down) + (dot(sh, rest, down) + dot(sl, high, down)))
        solved[:, lo:hi] = contract(value, inverses[k], ((1,), (0,)))
    for i in range(steps):
        for j in range(steps):
            factor[pl.ds(i * each * steps + j, each, stride=steps), :] = low[j, pl.ds(i * BW + me, each, stride=count), :]

    def extra(t, carry):
        tick(t)
        return carry

    lax.fori_loop(AHEAD + 3 * steps, 2 * bits + 2 + 4 * (chunks // 2 - 1) + 1, extra, 0)
    for c in range(chunks - 2, chunks):
        bot_relay(bits - 1, c).wait()
        bot_done(c)
    for at in range(0, panel, 2 * BW):
        right = jnp.concatenate([full[k, at : at + 2 * BW, :] for k in range(steps)], axis=1)
        change = contract(solved[...], right, ((1,), (1,)))
        for q in range(2):
            trail[at // BW + q] -= change[:, q * BW : (q + 1) * BW]

    lifted(bits - 1)
    for i in range(blocks - steps):
        for j in range(blocks - steps):
            value = trail[j, i * each : (i + 1) * each, :]
            if j > i:
                value = value + uppers[spot * number + triangle(j - 1) + i]
            trailing[pl.ds(i * each * steps + j, each, stride=steps), :] = value


def panels(pieces, above, table, diag, touched):
    count, _, each, _ = pieces.shape
    rows_all = diag.shape[1]
    panel = rows_all // 2
    steps = panel // BW
    own = panel // count
    bits = count.bit_length() - 1
    rows = panel + -(-own // 16) * 16
    dma = pltpu.SemaphoreType.DMA
    room = triangle(touched) + touched + 1 + triangle(touched) + 1
    blocks = rows_all // BW
    number = triangle(blocks - steps - 1)
    f32 = jnp.float32
    return pl.pallas_call(
        functools.partial(panel_kernel, count=count, touched=touched),
        out_shape=(
            jax.ShapeDtypeStruct((2 * own * steps, BW), f32),
            jax.ShapeDtypeStruct((own * steps, BW), f32),
        ),
        in_specs=[
            pl.BlockSpec(memory_space=pltpu.HBM),
            pl.BlockSpec(memory_space=pltpu.HBM),
            pl.BlockSpec(memory_space=pltpu.VMEM),
            pl.BlockSpec(memory_space=pltpu.VMEM),
        ],
        out_specs=(pl.BlockSpec(memory_space=pltpu.VMEM),) * 2,
        scratch_shapes=[
            pltpu.VMEM((count, room, each, BW), f32),
            pltpu.VMEM((count * number, each, BW), f32),
            pltpu.VMEM(((count - 1) * number, each, BW), f32),
            pltpu.VMEM((count, 1, BW), jnp.int32),
            pltpu.SMEM((count, 1, BW), jnp.int32),
            pltpu.VMEM((count * triangle(steps), each, BW), f32),
            pltpu.VMEM((count * steps * steps, each, BW), f32),
            pltpu.VMEM((steps, rows, BW), f32),
            pltpu.VMEM((steps, panel, BW), f32),
            pltpu.VMEM((steps, panel, BW), f32),
            pltpu.VMEM((steps, rows, BW), jnp.bfloat16),
            pltpu.VMEM((steps, rows, BW), jnp.bfloat16),
            pltpu.VMEM((steps, BW, BW), f32),
            pltpu.VMEM((own, panel), f32),
            pltpu.VMEM((blocks - steps, own, BW), f32),
        ]
        + [dma((count,))] * 4
        + [dma((bits,))] * 2
        + [dma((bits, steps))] * 2
        + [dma((bits, 8))] * 2
        + [dma((3,))],
        compiler_params=pltpu.CompilerParams(
            collective_id=0, has_side_effects=True, vmem_limit_bytes=60 * 1024 * 1024
        ),
        cost_estimate=pl.CostEstimate(flops=20_000_000_000, bytes_accessed=6_000_000, transcendentals=0),
        name="panels",
    )(pieces, above, table, diag)


def hand_kernel(factor, trailing, factor_out, trailing_out, done):
    copies = [
        pltpu.make_async_copy(factor, factor_out, done.at[0]),
        pltpu.make_async_copy(trailing, trailing_out, done.at[1]),
    ]
    for copy in copies:
        copy.start()
    for copy in copies:
        copy.wait()


def hand(factor, trailing):
    return pl.pallas_call(
        hand_kernel,
        out_shape=tuple(jax.ShapeDtypeStruct(a.shape, a.dtype) for a in (factor, trailing)),
        in_specs=[pl.BlockSpec(memory_space=pltpu.VMEM)] * 2,
        out_specs=(pl.BlockSpec(memory_space=pltpu.HBM),) * 2,
        scratch_shapes=[pltpu.SemaphoreType.DMA((2,))],
        name="hand",
    )(factor, trailing)


def shards(scenario_rows, barrier, blocks, link_diag):
    count = lax.axis_size("scen")
    pieces, above, table = gram(scenario_rows[0], barrier, blocks, count)
    factor, trailing = panels(pieces, above, table, link_diag[None, :], blocks.shape[1])
    factor, trailing = hand(factor, trailing)
    panel = link_diag.shape[0] // 2
    return (factor.reshape(-1, 1, panel), trailing.reshape(-1, 1, panel))


def solution(mesh):
    return jax.shard_map(
        shards,
        mesh=mesh,
        in_specs=(
            P(("group", "scen"), None, None),
            P(("group", "scen"), None),
            P(("group", "scen"), None),
            P("group"),
        ),
        out_specs=(P("group", "scen", None), P("group", "scen", None)),
        check_vma=False,
    )
```
